32 devices in a mesh: layer: 4 (over y, x), width: 8 (over z, core).
Axes of the slice: x: 2, y: 2, z: 4, core: 2. Of those that a mesh axis runs over, the one named last changes fastest.
Arguments:
- source: bfloat16 [4, 4096, 4096], P('layer', 'width'), may hold values from -6 to 6
- expand_out: bfloat16 [2560, 4096], P(None, 'width'), may hold values from -0.125 to 0.125
- expand_in: bfloat16 [2560, 4096], P(('layer', 'width')), may hold values from -0.09375 to 0.09375
- depth: float32 [8, 4], P('layer'), may hold values from -1.4 to 1.4
Outputs:
- grown: float32 [8, 2560, 2560], P('layer', 'width')
The draws below stay inside these ranges and needn't reach their ends.
All inputs are finite; a program needn't handle non-finite values.
Results may differ from the reference program's by a relative error of at most 0.018.
Values may be sent and summed in bfloat16 or wider, within the bound.
No kernel may reach another device: no remote copies, remote signals or barrier semaphores. Data moves between devices by JAX's collectives and lax.ppermute only.
A program may use at most 128 MiB of HBM per device.

```python
import jax
import jax.numpy as jnp
from jax import lax

D1 = 4096
R = 2560
C = 2560
SRC = 4
TGT = 8
N_WIDTH = 8


def spiked(values, own_key, source, target, blocks, factor):
    def block_of(axis_at):
        return (jnp.arange(values.shape[axis_at]) // (values.shape[axis_at] // blocks)).reshape((-1,) + (1,) * (values.ndim - 1 - axis_at))

    one_side = jax.random.permutation(own_key, blocks)[block_of(target)]
    other_side = (block_of(target) + blocks // 2) % blocks
    return jnp.where((block_of(source) == one_side) | (block_of(source) == other_side), factor * values, values)


def shard_levels(stream_key, extent, split, smallest, largest):
    def one(axis_at, parts):
        heights = jax.random.uniform(jax.random.fold_in(jax.random.fold_in(stream_key, 6), axis_at), (parts,), jnp.float32, smallest / len(split), largest / len(split))
        return jnp.repeat(jnp.exp(heights), extent[axis_at] // parts).reshape((-1,) + (1,) * (len(extent) - axis_at - 1))

    gain = one(*split[0])
    for cut in split[1:]:
        gain = gain * one(*cut)
    return gain


def centred(rng, shape, spread, reach, pieces=(), dtype=jnp.bfloat16):
    loudness = shard_levels(rng, shape, pieces, -0.22, 0.18) if pieces else 1.0
    values = jax.random.normal(rng, shape, jnp.float32) * spread * loudness
    return jnp.minimum(jnp.maximum(values, -reach), reach).astype(dtype)


def bell_draw_with(own_key, shape, deviation, most, cuts, heavy, held_as=jnp.bfloat16):
    values = deviation * jax.random.normal(own_key, shape, jnp.float32)
    if cuts:
        values = values * shard_levels(own_key, shape, cuts, -0.22, 0.18)
    return jnp.clip(spiked(values, jax.random.fold_in(own_key, 3), *heavy), -most, most).astype(held_as)


def setup_inputs(seed: int = 0) -> dict:
    streams_of = jax.random.split(jax.random.key(seed), 5)
    return {
        "source": centred(streams_of[0], (SRC, D1, D1), 1.0, 6.0, ((0, 4), (1, 8))),
        "expand_out": bell_draw_with(streams_of[1], (R, D1), D1 ** -0.5, 0.125, ((1, 8),), (1, 0, 8, 2.0)),
        "expand_in": centred(streams_of[2], (C, D1), D1 ** -0.5, 0.09375, ((0, 32),)),
        "depth": centred(streams_of[3], (TGT, SRC), 0.35, 1.4, ((0, 4),), jnp.float32),
    }


def reference(source, expand_out, expand_in, depth):
    block_count = N_WIDTH
    block_width = D1 // block_count

    def expand(weight):
        projected = jnp.dot(weight, expand_in.T, preferred_element_type=jnp.float32).astype(jnp.bfloat16)

        def add_block(block_index, running):
            first_row = (block_index * block_width).astype(jnp.int32)
            inner_rows = lax.dynamic_slice_in_dim(projected, first_row, block_width, 0)
            outer_cols = lax.dynamic_slice_in_dim(expand_out, first_row, block_width, 1)
            partial_value = jnp.dot(outer_cols, inner_rows, preferred_element_type=jnp.float32).astype(jnp.bfloat16)
            partial_value = lax.optimization_barrier(partial_value)
            return running + partial_value.astype(jnp.float32)

        running = lax.fori_loop(0, block_count, add_block, jnp.zeros((R, C), jnp.float32))
        return running.astype(jnp.bfloat16)

    expanded = lax.map(expand, source)
    stacked = expanded.astype(jnp.float32).reshape(SRC, R * C)
    grown = jnp.dot(depth, stacked, precision=lax.Precision.HIGHEST, preferred_element_type=jnp.float32)
    return grown.reshape(TGT, R, C)
```

```python
import jax
import jax.numpy as jnp
from jax import lax
from jax.experimental import pallas as pl
from jax.experimental.pallas import tpu as pltpu
from jax.sharding import PartitionSpec as P

AXES = ("layer", "width")
GROUPS = (1, 2, 2)
LANES = 128
PACK = 16


def splits(total, parts):
    edges = [total * p // parts for p in range(parts + 1)]
    return list(zip(edges[:-1], edges[1:]))


class Moves:
    def __init__(self, layers, chips, cores):
        self.layers, self.chips, self.cores = layers, chips, cores

    def send(self, value, target, senders=None):
        pairs = []
        for k in range(self.layers):
            for z in range(self.chips):
                for c in range(self.cores):
                    if senders is not None and z not in senders:
                        continue
                    pairs.append((self.at(k, z, c), self.at(*target(k, z, c))))
        return lax.ppermute(value, AXES, pairs)

    def at(self, k, z, c):
        return (k * self.chips + z) * self.cores + c

    def partner(self, value):
        return self.send(value, lambda k, z, c: (k, z, self.cores - 1 - c))

    def across(self, value, bit):
        return self.send(value, lambda k, z, c: (k ^ (1 << bit), z, c))

    def up(self, value, senders):
        return self.send(value, lambda k, z, c: (k, z + 1, c), senders)

    def down(self, value, senders):
        return self.send(value, lambda k, z, c: (k, z - 1, c), senders)


def line_gather(moves, own, z):
    n = moves.chips
    low, high = [own], [own]
    for hop in range(1, n):
        low.append(moves.up(low[-1], range(hop - 1, n - 1)))
        high.append(moves.down(high[-1], range(1, n - hop + 1)))
    blocks = []
    for b in range(n):
        held = own
        for at in range(n):
            if at > b:
                held = jnp.where(z == at, low[at - b], held)
            elif at < b:
                held = jnp.where(z == at, high[b - at], held)
        blocks.append(held)
    return jnp.concatenate(blocks, axis=0)


def cube_gather(moves, own):
    bits = moves.layers.bit_length() - 1
    held = {0: own}
    for weight in range(1, bits + 1):
        fresh = {}
        for rel in range(1, moves.layers):
            ways = [b for b in range(bits) if rel >> b & 1]
            if len(ways) != weight:
                continue
            parts = []
            for bit, (lo, hi) in zip(reversed(ways), splits(own.shape[0], weight)):
                parts.append(moves.across(held[rel ^ (1 << bit)][lo:hi], bit))
            fresh[rel] = parts[0] if weight == 1 else jnp.concatenate(parts, axis=0)
        held.update(fresh)
    return [held[rel] for rel in range(moves.layers)]


def line_scatter(moves, terms, z):
    n = moves.chips
    pick = lambda b: lax.dynamic_index_in_dim(terms, jnp.clip(b, 0, n - 1), 0, keepdims=False)
    add = lambda a, b: (a.astype(jnp.float32) + b.astype(jnp.float32)).astype(jnp.bfloat16)
    from_low = from_high = None
    for hop in range(1, n):
        low, high = pick(n + z - hop), pick(z + hop - n)
        if hop > 1:
            low, high = add(low, from_low), add(high, from_high)
        from_low = moves.up(low, range(0, hop))
        from_high = moves.down(high, range(n - hop, n))
    own = pick(z).astype(jnp.float32)
    return (own + from_low.astype(jnp.float32) + from_high.astype(jnp.float32)).astype(jnp.bfloat16)


def mm(a, b):
    return lax.dot_general(a, b, (((1,), (1,)), ((), ())), preferred_element_type=jnp.float32)


def spread_plan(source, expand_out, expand_in, depth):
    cores = 2
    layers, width = lax.axis_size("layer"), lax.axis_size("width")
    chips = width // cores
    moves = Moves(layers, chips, cores)
    me, w = lax.axis_index("layer"), lax.axis_index("width")
    z, core = w // cores, w % cores
    rows = expand_out.shape[0]
    own_rows = rows // width
    chip_rows = rows // chips
    mine = source.reshape(source.shape[0] * source.shape[1], source.shape[2])
    theirs = moves.partner(mine)
    out_mine = expand_out
    out_theirs = moves.partner(expand_out)
    held = expand_in.shape[0]
    window = -(-own_rows // LANES) * LANES
    if window > chip_rows:
        window = own_rows
    first = chip_rows - window

    if held % (PACK * sum(GROUPS)) == 0:
        unit = held // sum(GROUPS)
        edges = [0]
        for g in GROUPS:
            edges.append(edges[-1] + g * unit)
    else:
        edges = [0, held]

    pieces = []
    for lo, hi in zip(edges[:-1], edges[1:]):
        block = line_gather(moves, expand_in[lo:hi], z)
        chunk = jnp.concatenate(cube_gather(moves, block), axis=0)
        left = mm(chunk, mine).astype(jnp.bfloat16)
        right = mm(chunk, theirs).astype(jnp.bfloat16)
        terms = (mm(left, out_mine) + mm(right, out_theirs)).astype(jnp.bfloat16)
        terms = terms.reshape(terms.shape[0], chips, chip_rows).transpose(1, 0, 2)
        expanded = line_scatter(moves, terms, z)
        spread = jnp.stack(cube_gather(moves, expanded))
        keep = jnp.where(core == 0, spread[..., :window], spread[..., first:])
        give = jnp.where(core == 0, spread[..., first:], spread[..., :window])
        pieces.append((keep, moves.partner(give), hi - lo))

    by_core = []
    for which in range(cores):
        parts = [
            jnp.where(core == which, keep, got).reshape(layers, layers, chips, h, window)
            for keep, got, h in pieces
        ]
        by_core.append(jnp.concatenate(parts, axis=3))
    full = jnp.stack(by_core, axis=3)
    offset = jnp.where(core == 0, 0, own_rows - first)
    full = lax.dynamic_slice_in_dim(full, offset, own_rows, 5).astype(jnp.float32)
    grown = []
    index = jnp.arange(layers)
    for target in range(layers):
        col = full[index, index ^ me ^ target]
        weight = depth[:, index ^ me]
        grown.append(jnp.einsum("td,dznhr->trznh", weight, col, precision=lax.Precision.HIGHEST).reshape(depth.shape[0], own_rows, -1))
    return jnp.concatenate(grown, axis=2)


NT = (((1,), (1,)), ((), ()))

PIECES = (((0, 0),), ((0, 1), (1, 0)), ((2, 0), (1, 1)), ((2, 1), (3, 0)), ((3, 1),))


def project(units, h, inner, mine, theirs):
    depth = mine.shape[1]
    n = len(units)
    flat = [x for unit in units for x in unit]
    held = mine.shape[0]
    tile = min(256, held)
    steps = held // tile
    c = 2 * n * h

    def kernel(inner_ref, *refs):
        e, (own_ref, far_ref, out_ref, lhs) = refs[: 3 * n], refs[3 * n :]
        step = pl.program_id(0)

        @pl.when(step == 0)
        def _():
            for u in range(n):
                a, b, third = e[3 * u : 3 * u + 3]

                low = pl.ds(pl.multiple_of(2 * u * h + inner_ref[1] * h, PACK), h)
                high = pl.ds(pl.multiple_of((2 * u + 1) * h - inner_ref[1] * h, PACK), h)

                if a is b:
                    lhs[low, :] = a[...]
                else:

                    @pl.when(inner_ref[0] == 1)
                    def _():
                        lhs[low, :] = a[...]

                    @pl.when(inner_ref[0] == 0)
                    def _():
                        lhs[low, :] = b[...]

                lhs[high, :] = third[...]

        @pl.when(step < steps)
        def _():
            out_ref[...] = lax.dot_general(lhs[...], own_ref[...], NT, preferred_element_type=jnp.float32).astype(jnp.bfloat16)

        @pl.when(step >= steps)
        def _():
            out_ref[...] = lax.dot_general(lhs[...], far_ref[...], NT, preferred_element_type=jnp.float32).astype(jnp.bfloat16)

    return pl.pallas_call(
        kernel,
        grid_spec=pltpu.PrefetchScalarGridSpec(
            num_scalar_prefetch=1,
            grid=(2 * steps,),
            in_specs=[pl.BlockSpec((h, depth), lambda i, s: (0, 0), pipeline_mode=pl.Buffered(1))] * len(flat)
            + [
                pl.BlockSpec((tile, depth), lambda i, s: (jnp.minimum(i, steps - 1), 0)),
                pl.BlockSpec((tile, depth), lambda i, s: (jnp.maximum(i - steps, 0), 0)),
            ],
            out_specs=pl.BlockSpec((c, tile), lambda i, s: (0, i)),
            scratch_shapes=[pltpu.VMEM((c, depth), jnp.bfloat16)],
        ),
        out_shape=jax.ShapeDtypeStruct((c, 2 * held), jnp.bfloat16),
        compiler_params=pltpu.CompilerParams(vmem_limit_bytes=22 << 20, dimension_semantics=("arbitrary",)),
        cost_estimate=pl.CostEstimate(
            flops=4 * c * depth * held,
            bytes_accessed=2 * (c * depth + 2 * held * depth + 2 * c * held),
            transcendentals=0,
        ),
        name="project",
    )(inner, *flat, mine, theirs)


def expand(order, near, outs, chip_rows):
    c, depth = near.shape
    half = depth // 2
    steps = 4

    def kernel(order_ref, near_ref, own_ref, far_ref, give_ref, keep_ref):
        got = lax.dot_general(near_ref[:, :half], own_ref[...], NT, preferred_element_type=jnp.float32)
        got += lax.dot_general(near_ref[:, half:], far_ref[...], NT, preferred_element_type=jnp.float32)
        got = got.astype(jnp.bfloat16)
        step = pl.program_id(0)

        @pl.when(step < 2)
        def _():
            give_ref[0] = got

        @pl.when(step >= 2)
        def _():
            keep_ref[0] = got

    return pl.pallas_call(
        kernel,
        grid_spec=pltpu.PrefetchScalarGridSpec(
            num_scalar_prefetch=1,
            grid=(steps,),
            in_specs=[
                pl.BlockSpec((c, depth), lambda i, o: (0, 0)),
                pl.BlockSpec((chip_rows, half), lambda i, o: (o[i], 0)),
                pl.BlockSpec((chip_rows, half), lambda i, o: (o[i], 0)),
            ],
            out_specs=[
                pl.BlockSpec((1, c, chip_rows), lambda i, o: (jnp.minimum(i, 1), 0, 0)),
                pl.BlockSpec((1, c, chip_rows), lambda i, o: (jnp.maximum(i - 2, 0), 0, 0)),
            ],
        ),
        out_shape=[jax.ShapeDtypeStruct((2, c, chip_rows), jnp.bfloat16)] * 2,
        compiler_params=pltpu.CompilerParams(vmem_limit_bytes=12 << 20, dimension_semantics=("arbitrary",)),
        cost_estimate=pl.CostEstimate(
            flops=2 * c * depth * chip_rows * steps,
            bytes_accessed=2 * (c * depth + steps * (chip_rows * depth + c * chip_rows)),
            transcendentals=0,
        ),
        name="expand",
    )(order, near, *outs)


def hand_over(start, parts, counts, window):
    width = window // LANES
    c = parts[0].shape[0]
    sources = sum(counts) // c

    def kernel(start_ref, *refs):
        out_ref = refs[-1]
        row = 0
        for ref in refs[:-1]:
            n = ref.shape[0]
            out_ref[row // c, row % c : row % c + n, :] = ref[...]
            row += n

    return pl.pallas_call(
        kernel,
        grid_spec=pltpu.PrefetchScalarGridSpec(
            num_scalar_prefetch=1,
            grid=(width,),
            in_specs=[pl.BlockSpec((n, LANES), lambda i, s: (0, s[0] + i)) for n in counts],
            out_specs=pl.BlockSpec((sources, c, LANES), lambda i, s: (0, 0, i)),
        ),
        out_shape=jax.ShapeDtypeStruct((sources, c, window), parts[0].dtype),
        compiler_params=pltpu.CompilerParams(vmem_limit_bytes=8 << 20, dimension_semantics=("arbitrary",)),
        cost_estimate=pl.CostEstimate(flops=0, bytes_accessed=4 * sources * c * window, transcendentals=0),
        name="hand_over",
    )(start, *parts)


def mix(info, weight, kept, given, own_rows, window, first, held, columns):
    sources = given[0].shape[0]
    rels = sources
    counts = [[part.shape[0] for part in row] for row in kept]
    flat_parts = [part for row in kept for part in row]
    unit = 2 * held
    slots = 4
    targets = weight.shape[0]
    tall = 2 * slots * held
    pieces = len(PIECES)

    def kernel(info_ref, w_ref, *refs):
        total = len(flat_parts)
        flat = refs[:total]
        got = refs[total : total + pieces]
        out_ref, own, other, acc, turned, sems = refs[total + pieces :]
        step = pl.program_id(0)
        me, core = info_ref[0], info_ref[1]
        lane = pl.multiple_of(core * first, LANES)

        def copies(ring):
            for p, units in enumerate(PIECES):
                for u, (rel, kind) in enumerate(units):
                    for d in range(sources):
                        if rel ^ d != ring:
                            continue
                        yield pltpu.make_async_copy(
                            got[p].at[d, pl.ds(u * unit, unit)],
                            other.at[rel, d, pl.ds(kind * unit, unit)],
                            sems.at[ring],
                        )
                        want = d * len(units) * unit + u * unit
                        row = 0
                        for k, n in enumerate(counts[p]):
                            lo, hi = max(want, row), min(want + unit, row + n)
                            if lo < hi:
                                yield pltpu.make_async_copy(
                                    flat[sum(map(len, counts[:p])) + k].at[pl.ds(lo - row, hi - lo), pl.ds(lane, window)],
                                    own.at[rel, d, pl.ds(kind * unit + lo - want, hi - lo)],
                                    sems.at[ring],
                                )
                            row += n

        @pl.when(step == 0)
        def _():
            for ring in range(rels):
                for copy in copies(ring):
                    copy.start()

        for ring in range(rels):

            @pl.when(step == ring)
            def _():
                for copy in copies(ring):
                    copy.wait()

        for s in range(slots):
            z = info_ref[2 + s]
            for which in range(2):
                held_at = own if which == 0 else other
                base = z * unit + (core if which == 0 else 1 - core) * held
                base = pl.multiple_of(base, PACK)
                sums = [None] * targets
                for d in range(sources):
                    rel = step ^ d
                    value = held_at[rel, d, s * held : (s + 1) * held, :].astype(jnp.float32)
                    for t in range(targets):
                        term = value * w_ref[t, me ^ d]
                        sums[t] = term if d == 0 else sums[t] + term
                for t in range(targets):
                    acc[t, pl.ds(base, held), :] = sums[t]
        shift = pl.multiple_of(core * (own_rows - first), PACK)
        for t in range(targets):
            turned[...] = acc[t].T
            out_ref[t] = turned[pl.ds(shift, own_rows), :]

    return pl.pallas_call(
        kernel,
        grid_spec=pltpu.PrefetchScalarGridSpec(
            num_scalar_prefetch=2,
            grid=(rels,),
            in_specs=[pl.BlockSpec(memory_space=pl.ANY)] * (len(flat_parts) + pieces),
            out_specs=pl.BlockSpec((targets, own_rows, tall), lambda i, a, b: (0, 0, i ^ a[0])),
            scratch_shapes=[
                pltpu.VMEM((rels, sources, slots * held, window), jnp.bfloat16),
                pltpu.VMEM((rels, sources, slots * held, window), jnp.bfloat16),
                pltpu.VMEM((targets, tall, window), jnp.float32),
                pltpu.VMEM((window, tall), jnp.float32),
                pltpu.SemaphoreType.DMA((rels,)),
            ],
        ),
        out_shape=jax.ShapeDtypeStruct((targets, own_rows, columns), jnp.float32),
        compiler_params=pltpu.CompilerParams(dimension_semantics=("arbitrary",)),
        name="mix",
    )(info, weight, *flat_parts, *given)


def fold_plan(source, expand_out, expand_in, depth):
    cores = 2
    layers, width = lax.axis_size("layer"), lax.axis_size("width")
    chips = width // cores
    moves = Moves(layers, chips, cores)
    me, w = lax.axis_index("layer"), lax.axis_index("width")
    z, core = w // cores, w % cores
    rows, columns = expand_out.shape[0], expand_in.shape[0] * layers * width
    own_rows, chip_rows = rows // width, rows // chips
    window = -(-own_rows // LANES) * LANES
    first = chip_rows - window
    h = expand_in.shape[0]
    right = z >= chips // 2
    inner = jnp.logical_and(z > 0, z < chips - 1)

    pair = lambda v: moves.send(v, lambda k, z, c: (k, z ^ 1, c))
    middle = lambda v: moves.send(v, lambda k, z, c: (k, 3 - z if z in (1, 2) else z, c))
    mirror = lambda v: moves.send(v, lambda k, z, c: (k, 3 - z, c))
    over_x = lambda v: moves.across(v, 0)
    over_y = lambda v: moves.across(v, 1)
    partner = moves.partner

    mine = source.reshape(source.shape[0] * source.shape[1], source.shape[2])
    own = expand_in
    near_z = pair(own)
    mid_a = middle(own)
    x0, y0 = over_x(own), over_y(own)
    theirs = partner(mine)
    outs = (expand_out, partner(expand_out))
    mid_b = middle(near_z)
    out_b = pair(mid_a)
    x1, y1 = over_x(near_z), over_y(near_z)
    choose = lambda a, b: jnp.where(inner, a, b)
    third = choose(mid_a, out_b)
    out_c = pair(mid_b)
    x2, y2 = over_x(third), over_y(third)
    fourth = choose(mid_b, out_c)
    x3, y3 = over_x(fourth), over_y(fourth)
    d0, d2 = over_x(jnp.where(inner, y0, y1)), over_y(x2)
    d1, d3 = over_x(jnp.where(inner, y1, y0)), over_y(x3)
    held = [(own, near_z, third, fourth), (x0, x1, x2, x3), (y0, y1, y2, y3)]

    def unit(rel, kind):
        if rel == 3:
            return (d0, d0, d2) if kind == 0 else (d1, d1, d3)
        a, b, c, d = held[rel]
        return (a, b, c) if kind == 0 else (b, a, d)

    flip = lambda m: jnp.where(right, chips - 1 - m, m)
    ints = lambda *v: jnp.stack([jnp.asarray(x, jnp.int32) for x in v])
    order = ints(*[flip(jnp.where(inner, m, e)) for m, e in ((0, 1), (3, 2), (1, 0), (2, 3))])
    place = ints(inner, right)
    f32 = jnp.float32

    kept, given = [], []
    for piece in PIECES:
        near = project([unit(*u) for u in piece], h, place, mine, theirs)
        give, keep = expand(order, near, outs, chip_rows)
        got = pair(give)
        last = mirror((keep[1].astype(f32) + got[1].astype(f32)).astype(jnp.bfloat16))
        expanded = (keep[0].astype(f32) + got[0].astype(f32) + last.astype(f32)).astype(jnp.bfloat16)
        from_x, from_y = over_x(expanded), over_y(expanded)
        cut = expanded.shape[0] // 2
        low, high = over_x(from_y[:cut]), over_y(from_x[cut:])
        spread = [expanded, from_x, from_y, low, high]
        start = ints(jnp.where(core == 0, first // LANES, 0))
        give = hand_over(start, spread, [part.shape[0] for part in spread], window)
        kept.append(spread)
        given.append(partner(give))

    info = ints(me, core, 1, 2, 0, 3)
    return mix(info, depth, kept, given, own_rows, window, first, h, columns)


def on_device(source, expand_out, expand_in, depth):
    chips = lax.axis_size("width") // 2
    aligned = expand_in.shape[0] % PACK == 0 and expand_out.shape[0] % (chips * LANES) == 0
    plan = fold_plan if chips == 4 and lax.axis_size("layer") == 4 and aligned else spread_plan
    return plan(source, expand_out, expand_in, depth)


def solution(mesh):
    return jax.shard_map(
        on_device,
        mesh=mesh,
        in_specs=(
            P("layer", "width", None),
            P(None, "width"),
            P(("layer", "width"), None),
            P("layer", None),
        ),
        out_specs=P("layer", "width", None),
        check_vma=False,
    )
```

```python
import jax
import jax.numpy as jnp
from jax import lax
from jax.experimental import pallas as pl
from jax.experimental.pallas import tpu as pltpu
from jax.sharding import PartitionSpec as P

AXES = ("layer", "width")
GROUPS = (1, 2, 2)
LANES = 128
PACK = 16


def splits(total, parts):
    edges = [total * p // parts for p in range(parts + 1)]
    return list(zip(edges[:-1], edges[1:]))


class Moves:
    def __init__(self, layers, chips, cores):
        self.layers, self.chips, self.cores = layers, chips, cores

    def send(self, value, target, senders=None):
        pairs = []
        for k in range(self.layers):
            for z in range(self.chips):
                for c in range(self.cores):
                    if senders is not None and z not in senders:
                        continue
                    pairs.append((self.at(k, z, c), self.at(*target(k, z, c))))
        return lax.ppermute(value, AXES, pairs)

    def at(self, k, z, c):
        return (k * self.chips + z) * self.cores + c

    def partner(self, value):
        return self.send(value, lambda k, z, c: (k, z, self.cores - 1 - c))

    def across(self, value, bit):
        return self.send(value, lambda k, z, c: (k ^ (1 << bit), z, c))

    def up(self, value, senders):
        return self.send(value, lambda k, z, c: (k, z + 1, c), senders)

    def down(self, value, senders):
        return self.send(value, lambda k, z, c: (k, z - 1, c), senders)


def line_gather(moves, own, z):
    n = moves.chips
    low, high = [own], [own]
    for hop in range(1, n):
        low.append(moves.up(low[-1], range(hop - 1, n - 1)))
        high.append(moves.down(high[-1], range(1, n - hop + 1)))
    blocks = []
    for b in range(n):
        held = own
        for at in range(n):
            if at > b:
                held = jnp.where(z == at, low[at - b], held)
            elif at < b:
                held = jnp.where(z == at, high[b - at], held)
        blocks.append(held)
    return jnp.concatenate(blocks, axis=0)


def cube_gather(moves, own):
    bits = moves.layers.bit_length() - 1
    held = {0: own}
    for weight in range(1, bits + 1):
        fresh = {}
        for rel in range(1, moves.layers):
            ways = [b for b in range(bits) if rel >> b & 1]
            if len(ways) != weight:
                continue
            parts = []
            for bit, (lo, hi) in zip(reversed(ways), splits(own.shape[0], weight)):
                parts.append(moves.across(held[rel ^ (1 << bit)][lo:hi], bit))
            fresh[rel] = parts[0] if weight == 1 else jnp.concatenate(parts, axis=0)
        held.update(fresh)
    return [held[rel] for rel in range(moves.layers)]


def line_scatter(moves, terms, z):
    n = moves.chips
    pick = lambda b: lax.dynamic_index_in_dim(terms, jnp.clip(b, 0, n - 1), 0, keepdims=False)
    add = lambda a, b: (a.astype(jnp.float32) + b.astype(jnp.float32)).astype(jnp.bfloat16)
    from_low = from_high = None
    for hop in range(1, n):
        low, high = pick(n + z - hop), pick(z + hop - n)
        if hop > 1:
            low, high = add(low, from_low), add(high, from_high)
        from_low = moves.up(low, range(0, hop))
        from_high = moves.down(high, range(n - hop, n))
    own = pick(z).astype(jnp.float32)
    return (own + from_low.astype(jnp.float32) + from_high.astype(jnp.float32)).astype(jnp.bfloat16)


def mm(a, b):
    return lax.dot_general(a, b, (((1,), (1,)), ((), ())), preferred_element_type=jnp.float32)


def spread_plan(source, expand_out, expand_in, depth):
    cores = 2
    layers, width = lax.axis_size("layer"), lax.axis_size("width")
    chips = width // cores
    moves = Moves(layers, chips, cores)
    me, w = lax.axis_index("layer"), lax.axis_index("width")
    z, core = w // cores, w % cores
    rows = expand_out.shape[0]
    own_rows = rows // width
    chip_rows = rows // chips
    mine = source.reshape(source.shape[0] * source.shape[1], source.shape[2])
    theirs = moves.partner(mine)
    out_mine = expand_out
    out_theirs = moves.partner(expand_out)
    held = expand_in.shape[0]
    window = -(-own_rows // LANES) * LANES
    if window > chip_rows:
        window = own_rows
    first = chip_rows - window

    if held % (PACK * sum(GROUPS)) == 0:
        unit = held // sum(GROUPS)
        edges = [0]
        for g in GROUPS:
            edges.append(edges[-1] + g * unit)
    else:
        edges = [0, held]

    pieces = []
    for lo, hi in zip(edges[:-1], edges[1:]):
        block = line_gather(moves, expand_in[lo:hi], z)
        chunk = jnp.concatenate(cube_gather(moves, block), axis=0)
        left = mm(chunk, mine).astype(jnp.bfloat16)
        right = mm(chunk, theirs).astype(jnp.bfloat16)
        terms = (mm(left, out_mine) + mm(right, out_theirs)).astype(jnp.bfloat16)
        terms = terms.reshape(terms.shape[0], chips, chip_rows).transpose(1, 0, 2)
        expanded = line_scatter(moves, terms, z)
        spread = jnp.stack(cube_gather(moves, expanded))
        keep = jnp.where(core == 0, spread[..., :window], spread[..., first:])
        give = jnp.where(core == 0, spread[..., first:], spread[..., :window])
        pieces.append((keep, moves.partner(give), hi - lo))

    by_core = []
    for which in range(cores):
        parts = [
            jnp.where(core == which, keep, got).reshape(layers, layers, chips, h, window)
            for keep, got, h in pieces
        ]
        by_core.append(jnp.concatenate(parts, axis=3))
    full = jnp.stack(by_core, axis=3)
    offset = jnp.where(core == 0, 0, own_rows - first)
    full = lax.dynamic_slice_in_dim(full, offset, own_rows, 5).astype(jnp.float32)
    grown = []
    index = jnp.arange(layers)
    for target in range(layers):
        col = full[index, index ^ me ^ target]
        weight = depth[:, index ^ me]
        grown.append(jnp.einsum("td,dznhr->trznh", weight, col, precision=lax.Precision.HIGHEST).reshape(depth.shape[0], own_rows, -1))
    return jnp.concatenate(grown, axis=2)


NT = (((1,), (1,)), ((), ()))

PIECES = (((0, 0),), ((0, 1), (1, 0)), ((2, 0), (1, 1)), ((2, 1), (3, 0)), ((3, 1),))


def project(units, h, inner, mine, theirs):
    depth = mine.shape[1]
    n = len(units)
    flat = [x for unit in units for x in unit]
    held = mine.shape[0]
    tile = min(256, held)
    steps = held // tile
    c = 2 * n * h

    def kernel(inner_ref, *refs):
        e, (own_ref, far_ref, out_ref, lhs, sems) = refs[: 3 * n], refs[3 * n :]
        step = pl.program_id(0)

        @pl.when(step == 0)
        def _():
            for u in range(n):
                a, b, third = e[3 * u : 3 * u + 3]

                low = pl.ds(pl.multiple_of(2 * u * h + inner_ref[1] * h, PACK), h)
                high = pl.ds(pl.multiple_of((2 * u + 1) * h - inner_ref[1] * h, PACK), h)
                if a is b:
                    pltpu.make_async_copy(a, lhs.at[low], sems.at[2 * u]).start()
                else:

                    @pl.when(inner_ref[0] == 1)
                    def _():
                        pltpu.make_async_copy(a, lhs.at[low], sems.at[2 * u]).start()

                    @pl.when(inner_ref[0] == 0)
                    def _():
                        pltpu.make_async_copy(b, lhs.at[low], sems.at[2 * u]).start()

                pltpu.make_async_copy(third, lhs.at[high], sems.at[2 * u + 1]).start()
            for u in range(n):
                for part in range(2):
                    rows = pl.ds((2 * u + part) * h, h)
                    pltpu.make_async_copy(e[3 * u], lhs.at[rows], sems.at[2 * u + part]).wait()

        @pl.when(step < steps)
        def _():
            out_ref[...] = lax.dot_general(lhs[...], own_ref[...], NT, preferred_element_type=jnp.float32).astype(jnp.bfloat16)

        @pl.when(step >= steps)
        def _():
            out_ref[...] = lax.dot_general(lhs[...], far_ref[...], NT, preferred_element_type=jnp.float32).astype(jnp.bfloat16)

    return pl.pallas_call(
        kernel,
        grid_spec=pltpu.PrefetchScalarGridSpec(
            num_scalar_prefetch=1,
            grid=(2 * steps,),
            in_specs=[pl.BlockSpec(memory_space=pl.ANY)] * len(flat)
            + [
                pl.BlockSpec((tile, depth), lambda i, s: (jnp.minimum(i, steps - 1), 0)),
                pl.BlockSpec((tile, depth), lambda i, s: (jnp.maximum(i - steps, 0), 0)),
            ],
            out_specs=pl.BlockSpec((c, tile), lambda i, s: (0, i)),
            scratch_shapes=[pltpu.VMEM((c, depth), jnp.bfloat16), pltpu.SemaphoreType.DMA((2 * n,))],
        ),
        out_shape=jax.ShapeDtypeStruct((c, 2 * held), jnp.bfloat16),
        compiler_params=pltpu.CompilerParams(vmem_limit_bytes=20 << 20, dimension_semantics=("arbitrary",)),
        cost_estimate=pl.CostEstimate(
            flops=4 * c * depth * held,
            bytes_accessed=2 * (c * depth + 2 * held * depth + 2 * c * held),
            transcendentals=0,
        ),
        name="project",
    )(inner, *flat, mine, theirs)


def expand(order, near, outs, chip_rows):
    c, depth = near.shape
    half = depth // 2
    steps = 4

    def kernel(order_ref, near_ref, own_ref, far_ref, give_ref, keep_ref):
        got = lax.dot_general(near_ref[:, :half], own_ref[...], NT, preferred_element_type=jnp.float32)
        got += lax.dot_general(near_ref[:, half:], far_ref[...], NT, preferred_element_type=jnp.float32)
        got = got.astype(jnp.bfloat16)
        step = pl.program_id(0)

        @pl.when(step < 2)
        def _():
            give_ref[0] = got

        @pl.when(step >= 2)
        def _():
            keep_ref[0] = got

    return pl.pallas_call(
        kernel,
        grid_spec=pltpu.PrefetchScalarGridSpec(
            num_scalar_prefetch=1,
            grid=(steps,),
            in_specs=[
                pl.BlockSpec((c, depth), lambda i, o: (0, 0)),
                pl.BlockSpec((chip_rows, half), lambda i, o: (o[i], 0)),
                pl.BlockSpec((chip_rows, half), lambda i, o: (o[i], 0)),
            ],
            out_specs=[
                pl.BlockSpec((1, c, chip_rows), lambda i, o: (jnp.minimum(i, 1), 0, 0)),
                pl.BlockSpec((1, c, chip_rows), lambda i, o: (jnp.maximum(i - 2, 0), 0, 0)),
            ],
        ),
        out_shape=[jax.ShapeDtypeStruct((2, c, chip_rows), jnp.bfloat16)] * 2,
        compiler_params=pltpu.CompilerParams(vmem_limit_bytes=12 << 20, dimension_semantics=("arbitrary",)),
        cost_estimate=pl.CostEstimate(
            flops=2 * c * depth * chip_rows * steps,
            bytes_accessed=2 * (c * depth + steps * (chip_rows * depth + c * chip_rows)),
            transcendentals=0,
        ),
        name="expand",
    )(order, near, *outs)


def hand_over(start, parts, counts, window):
    width = window // LANES
    c = parts[0].shape[0]
    sources = sum(counts) // c

    def kernel(start_ref, *refs):
        out_ref = refs[-1]
        row = 0
        for ref in refs[:-1]:
            n = ref.shape[0]
            out_ref[row // c, row % c : row % c + n, :] = ref[...]
            row += n

    return pl.pallas_call(
        kernel,
        grid_spec=pltpu.PrefetchScalarGridSpec(
            num_scalar_prefetch=1,
            grid=(width,),
            in_specs=[pl.BlockSpec((n, LANES), lambda i, s: (0, s[0] + i)) for n in counts],
            out_specs=pl.BlockSpec((sources, c, LANES), lambda i, s: (0, 0, i)),
        ),
        out_shape=jax.ShapeDtypeStruct((sources, c, window), parts[0].dtype),
        compiler_params=pltpu.CompilerParams(vmem_limit_bytes=8 << 20, dimension_semantics=("arbitrary",)),
        cost_estimate=pl.CostEstimate(flops=0, bytes_accessed=4 * sources * c * window, transcendentals=0),
        name="hand_over",
    )(start, *parts)


def mix(info, weight, kept, given, own_rows, window, first, held, columns):
    sources = given[0].shape[0]
    rels = sources
    counts = [[part.shape[0] for part in row] for row in kept]
    flat_parts = [part for row in kept for part in row]
    unit = 2 * held
    slots = 4
    targets = weight.shape[0]
    tall = 2 * slots * held
    pieces = len(PIECES)

    def kernel(info_ref, w_ref, *refs):
        total = len(flat_parts)
        flat = refs[:total]
        got = refs[total : total + pieces]
        out_ref, own, other, acc, turned, sems = refs[total + pieces :]
        step = pl.program_id(0)
        me, core = info_ref[0], info_ref[1]
        lane = pl.multiple_of(core * first, LANES)

        def copies(ring):
            for p, units in enumerate(PIECES):
                for u, (rel, kind) in enumerate(units):
                    for d in range(sources):
                        if rel ^ d != ring:
                            continue
                        yield pltpu.make_async_copy(
                            got[p].at[d, pl.ds(u * unit, unit)],
                            other.at[rel, d, pl.ds(kind * unit, unit)],
                            sems.at[ring],
                        )
                        want = d * len(units) * unit + u * unit
                        row = 0
                        for k, n in enumerate(counts[p]):
                            lo, hi = max(want, row), min(want + unit, row + n)
                            if lo < hi:
                                yield pltpu.make_async_copy(
                                    flat[sum(map(len, counts[:p])) + k].at[pl.ds(lo - row, hi - lo), pl.ds(lane, window)],
                                    own.at[rel, d, pl.ds(kind * unit + lo - want, hi - lo)],
                                    sems.at[ring],
                                )
                            row += n

        @pl.when(step == 0)
        def _():
            for ring in range(rels):
                for copy in copies(ring):
                    copy.start()

        for ring in range(rels):

            @pl.when(step == ring)
            def _():
                for copy in copies(ring):
                    copy.wait()

        for s in range(slots):
            z = info_ref[2 + s]
            for which in range(2):
                held_at = own if which == 0 else other
                base = z * unit + (core if which == 0 else 1 - core) * held
                base = pl.multiple_of(base, PACK)
                sums = [None] * targets
                for d in range(sources):
                    rel = step ^ d
                    value = held_at[rel, d, s * held : (s + 1) * held, :].astype(jnp.float32)
                    for t in range(targets):
                        term = value * w_ref[t, me ^ d]
                        sums[t] = term if d == 0 else sums[t] + term
                for t in range(targets):
                    acc[t, pl.ds(base, held), :] = sums[t]
        shift = pl.multiple_of(core * (own_rows - first), PACK)
        for t in range(targets):
            turned[...] = acc[t].T
            out_ref[t] = turned[pl.ds(shift, own_rows), :]

    return pl.pallas_call(
        kernel,
        grid_spec=pltpu.PrefetchScalarGridSpec(
            num_scalar_prefetch=2,
            grid=(rels,),
            in_specs=[pl.BlockSpec(memory_space=pl.ANY)] * (len(flat_parts) + pieces),
            out_specs=pl.BlockSpec((targets, own_rows, tall), lambda i, a, b: (0, 0, i ^ a[0])),
            scratch_shapes=[
                pltpu.VMEM((rels, sources, slots * held, window), jnp.bfloat16),
                pltpu.VMEM((rels, sources, slots * held, window), jnp.bfloat16),
                pltpu.VMEM((targets, tall, window), jnp.float32),
                pltpu.VMEM((window, tall), jnp.float32),
                pltpu.SemaphoreType.DMA((rels,)),
            ],
        ),
        out_shape=jax.ShapeDtypeStruct((targets, own_rows, columns), jnp.float32),
        compiler_params=pltpu.CompilerParams(dimension_semantics=("arbitrary",)),
        name="mix",
    )(info, weight, *flat_parts, *given)


def fold_plan(source, expand_out, expand_in, depth):
    cores = 2
    layers, width = lax.axis_size("layer"), lax.axis_size("width")
    chips = width // cores
    moves = Moves(layers, chips, cores)
    me, w = lax.axis_index("layer"), lax.axis_index("width")
    z, core = w // cores, w % cores
    rows, columns = expand_out.shape[0], expand_in.shape[0] * layers * width
    own_rows, chip_rows = rows // width, rows // chips
    window = -(-own_rows // LANES) * LANES
    first = chip_rows - window
    h = expand_in.shape[0]
    right = z >= chips // 2
    inner = jnp.logical_and(z > 0, z < chips - 1)

    pair = lambda v: moves.send(v, lambda k, z, c: (k, z ^ 1, c))
    middle = lambda v: moves.send(v, lambda k, z, c: (k, 3 - z if z in (1, 2) else z, c))
    mirror = lambda v: moves.send(v, lambda k, z, c: (k, 3 - z, c))
    over_x = lambda v: moves.across(v, 0)
    over_y = lambda v: moves.across(v, 1)
    partner = moves.partner

    mine = source.reshape(source.shape[0] * source.shape[1], source.shape[2])
    own = expand_in
    near_z = pair(own)
    mid_a = middle(own)
    x0, y0 = over_x(own), over_y(own)
    theirs = partner(mine)
    outs = (expand_out, partner(expand_out))
    mid_b = middle(near_z)
    out_b = pair(mid_a)
    x1, y1 = over_x(near_z), over_y(near_z)
    choose = lambda a, b: jnp.where(inner, a, b)
    third = choose(mid_a, out_b)
    out_c = pair(mid_b)
    x2, y2 = over_x(third), over_y(third)
    fourth = choose(mid_b, out_c)
    x3, y3 = over_x(fourth), over_y(fourth)
    d0, d2 = over_x(jnp.where(inner, y0, y1)), over_y(x2)
    d1, d3 = over_x(jnp.where(inner, y1, y0)), over_y(x3)
    held = [(own, near_z, third, fourth), (x0, x1, x2, x3), (y0, y1, y2, y3)]

    def unit(rel, kind):
        if rel == 3:
            return (d0, d0, d2) if kind == 0 else (d1, d1, d3)
        a, b, c, d = held[rel]
        return (a, b, c) if kind == 0 else (b, a, d)

    flip = lambda m: jnp.where(right, chips - 1 - m, m)
    ints = lambda *v: jnp.stack([jnp.asarray(x, jnp.int32) for x in v])
    order = ints(*[flip(jnp.where(inner, m, e)) for m, e in ((0, 1), (3, 2), (1, 0), (2, 3))])
    place = ints(inner, right)
    f32 = jnp.float32

    kept, given = [], []
    for i, piece in enumerate(PIECES):
        near = project([unit(*u) for u in piece], h, place, mine, theirs)
        give, keep = expand(order, near, outs, chip_rows)
        got = pair(give)
        last = mirror((keep[1].astype(f32) + got[1].astype(f32)).astype(jnp.bfloat16))
        expanded = (keep[0].astype(f32) + got[0].astype(f32) + last.astype(f32)).astype(jnp.bfloat16)
        from_x, from_y = over_x(expanded), over_y(expanded)
        if i < len(PIECES) - 2:
            diagonal = [over_x(from_y) if i % 2 == 0 else over_y(from_x)]
        else:
            cut = expanded.shape[0] // 2
            diagonal = [over_x(from_y[:cut]), over_y(from_x[cut:])]
        spread = [expanded, from_x, from_y, *diagonal]
        start = ints(jnp.where(core == 0, first // LANES, 0))
        give = hand_over(start, spread, [part.shape[0] for part in spread], window)
        kept.append(spread)
        given.append(partner(give))

    info = ints(me, core, 1, 2, 0, 3)
    return mix(info, depth, kept, given, own_rows, window, first, h, columns)


def on_device(source, expand_out, expand_in, depth):
    chips = lax.axis_size("width") // 2
    aligned = expand_in.shape[0] % PACK == 0 and expand_out.shape[0] % (chips * LANES) == 0
    plan = fold_plan if chips == 4 and lax.axis_size("layer") == 4 and aligned else spread_plan
    return plan(source, expand_out, expand_in, depth)


def solution(mesh):
    return jax.shard_map(
        on_device,
        mesh=mesh,
        in_specs=(
            P("layer", "width", None),
            P(None, "width"),
            P(("layer", "width"), None),
            P("layer", None),
        ),
        out_specs=P("layer", "width", None),
        check_vma=False,
    )
```

```python
import jax
import jax.numpy as jnp
from jax import lax
from jax.experimental import pallas as pl
from jax.experimental.pallas import tpu as pltpu
from jax.sharding import PartitionSpec as P

AXES = ("layer", "width")
GROUPS = (1, 2, 2)
LANES = 128
PACK = 16


def splits(total, parts):
    edges = [total * p // parts for p in range(parts + 1)]
    return list(zip(edges[:-1], edges[1:]))


class Moves:
    def __init__(self, layers, chips, cores):
        self.layers, self.chips, self.cores = layers, chips, cores

    def send(self, value, target, senders=None):
        pairs = []
        for k in range(self.layers):
            for z in range(self.chips):
                for c in range(self.cores):
                    if senders is not None and z not in senders:
                        continue
                    pairs.append((self.at(k, z, c), self.at(*target(k, z, c))))
        return lax.ppermute(value, AXES, pairs)

    def at(self, k, z, c):
        return (k * self.chips + z) * self.cores + c

    def partner(self, value):
        return self.send(value, lambda k, z, c: (k, z, self.cores - 1 - c))

    def across(self, value, bit):
        return self.send(value, lambda k, z, c: (k ^ (1 << bit), z, c))

    def up(self, value, senders):
        return self.send(value, lambda k, z, c: (k, z + 1, c), senders)

    def down(self, value, senders):
        return self.send(value, lambda k, z, c: (k, z - 1, c), senders)


def line_gather(moves, own, z):
    n = moves.chips
    low, high = [own], [own]
    for hop in range(1, n):
        low.append(moves.up(low[-1], range(hop - 1, n - 1)))
        high.append(moves.down(high[-1], range(1, n - hop + 1)))
    blocks = []
    for b in range(n):
        held = own
        for at in range(n):
            if at > b:
                held = jnp.where(z == at, low[at - b], held)
            elif at < b:
                held = jnp.where(z == at, high[b - at], held)
        blocks.append(held)
    return jnp.concatenate(blocks, axis=0)


def cube_gather(moves, own):
    bits = moves.layers.bit_length() - 1
    held = {0: own}
    for weight in range(1, bits + 1):
        fresh = {}
        for rel in range(1, moves.layers):
            ways = [b for b in range(bits) if rel >> b & 1]
            if len(ways) != weight:
                continue
            parts = []
            for bit, (lo, hi) in zip(reversed(ways), splits(own.shape[0], weight)):
                parts.append(moves.across(held[rel ^ (1 << bit)][lo:hi], bit))
            fresh[rel] = parts[0] if weight == 1 else jnp.concatenate(parts, axis=0)
        held.update(fresh)
    return [held[rel] for rel in range(moves.layers)]


def line_scatter(moves, terms, z):
    n = moves.chips
    pick = lambda b: lax.dynamic_index_in_dim(terms, jnp.clip(b, 0, n - 1), 0, keepdims=False)
    add = lambda a, b: (a.astype(jnp.float32) + b.astype(jnp.float32)).astype(jnp.bfloat16)
    from_low = from_high = None
    for hop in range(1, n):
        low, high = pick(n + z - hop), pick(z + hop - n)
        if hop > 1:
            low, high = add(low, from_low), add(high, from_high)
        from_low = moves.up(low, range(0, hop))
        from_high = moves.down(high, range(n - hop, n))
    own = pick(z).astype(jnp.float32)
    return (own + from_low.astype(jnp.float32) + from_high.astype(jnp.float32)).astype(jnp.bfloat16)


def mm(a, b):
    return lax.dot_general(a, b, (((1,), (1,)), ((), ())), preferred_element_type=jnp.float32)


def spread_plan(source, expand_out, expand_in, depth):
    cores = 2
    layers, width = lax.axis_size("layer"), lax.axis_size("width")
    chips = width // cores
    moves = Moves(layers, chips, cores)
    me, w = lax.axis_index("layer"), lax.axis_index("width")
    z, core = w // cores, w % cores
    rows = expand_out.shape[0]
    own_rows = rows // width
    chip_rows = rows // chips
    mine = source.reshape(source.shape[0] * source.shape[1], source.shape[2])
    theirs = moves.partner(mine)
    out_mine = expand_out
    out_theirs = moves.partner(expand_out)
    held = expand_in.shape[0]
    window = -(-own_rows // LANES) * LANES
    if window > chip_rows:
        window = own_rows
    first = chip_rows - window

    if held % (PACK * sum(GROUPS)) == 0:
        unit = held // sum(GROUPS)
        edges = [0]
        for g in GROUPS:
            edges.append(edges[-1] + g * unit)
    else:
        edges = [0, held]

    pieces = []
    for lo, hi in zip(edges[:-1], edges[1:]):
        block = line_gather(moves, expand_in[lo:hi], z)
        chunk = jnp.concatenate(cube_gather(moves, block), axis=0)
        left = mm(chunk, mine).astype(jnp.bfloat16)
        right = mm(chunk, theirs).astype(jnp.bfloat16)
        terms = (mm(left, out_mine) + mm(right, out_theirs)).astype(jnp.bfloat16)
        terms = terms.reshape(terms.shape[0], chips, chip_rows).transpose(1, 0, 2)
        expanded = line_scatter(moves, terms, z)
        spread = jnp.stack(cube_gather(moves, expanded))
        keep = jnp.where(core == 0, spread[..., :window], spread[..., first:])
        give = jnp.where(core == 0, spread[..., first:], spread[..., :window])
        pieces.append((keep, moves.partner(give), hi - lo))

    by_core = []
    for which in range(cores):
        parts = [
            jnp.where(core == which, keep, got).reshape(layers, layers, chips, h, window)
            for keep, got, h in pieces
        ]
        by_core.append(jnp.concatenate(parts, axis=3))
    full = jnp.stack(by_core, axis=3)
    offset = jnp.where(core == 0, 0, own_rows - first)
    full = lax.dynamic_slice_in_dim(full, offset, own_rows, 5).astype(jnp.float32)
    grown = []
    index = jnp.arange(layers)
    for target in range(layers):
        col = full[index, index ^ me ^ target]
        weight = depth[:, index ^ me]
        grown.append(jnp.einsum("td,dznhr->trznh", weight, col, precision=lax.Precision.HIGHEST).reshape(depth.shape[0], own_rows, -1))
    return jnp.concatenate(grown, axis=2)


NT = (((1,), (1,)), ((), ()))

PIECES = (((0, 0),), ((0, 1), (1, 0)), ((2, 0), (1, 1)), ((2, 1), (3, 0)), ((3, 1),))


def project(units, h, inner, mine, theirs):
    depth = mine.shape[1]
    n = len(units)
    flat = [x for unit in units for x in unit]
    held = mine.shape[0]
    tile = min(256, held)
    steps = held // tile
    c = 2 * n * h

    def kernel(inner_ref, *refs):
        e, (own_ref, far_ref, out_ref, lhs, sems) = refs[: 3 * n], refs[3 * n :]
        step = pl.program_id(0)

        @pl.when(step == 0)
        def _():
            for u in range(n):
                a, b, third = e[3 * u : 3 * u + 3]

                low = pl.ds(pl.multiple_of(2 * u * h + inner_ref[1] * h, PACK), h)
                high = pl.ds(pl.multiple_of((2 * u + 1) * h - inner_ref[1] * h, PACK), h)
                if a is b:
                    pltpu.make_async_copy(a, lhs.at[low], sems.at[2 * u]).start()
                else:

                    @pl.when(inner_ref[0] == 1)
                    def _():
                        pltpu.make_async_copy(a, lhs.at[low], sems.at[2 * u]).start()

                    @pl.when(inner_ref[0] == 0)
                    def _():
                        pltpu.make_async_copy(b, lhs.at[low], sems.at[2 * u]).start()

                pltpu.make_async_copy(third, lhs.at[high], sems.at[2 * u + 1]).start()
            for u in range(n):
                for part in range(2):
                    rows = pl.ds((2 * u + part) * h, h)
                    pltpu.make_async_copy(e[3 * u], lhs.at[rows], sems.at[2 * u + part]).wait()

        @pl.when(step < steps)
        def _():
            out_ref[...] = lax.dot_general(lhs[...], own_ref[...], NT, preferred_element_type=jnp.float32).astype(jnp.bfloat16)

        @pl.when(step >= steps)
        def _():
            out_ref[...] = lax.dot_general(lhs[...], far_ref[...], NT, preferred_element_type=jnp.float32).astype(jnp.bfloat16)

    return pl.pallas_call(
        kernel,
        grid_spec=pltpu.PrefetchScalarGridSpec(
            num_scalar_prefetch=1,
            grid=(2 * steps,),
            in_specs=[pl.BlockSpec(memory_space=pl.ANY)] * len(flat)
            + [
                pl.BlockSpec((tile, depth), lambda i, s: (jnp.minimum(i, steps - 1), 0)),
                pl.BlockSpec((tile, depth), lambda i, s: (jnp.maximum(i - steps, 0), 0)),
            ],
            out_specs=pl.BlockSpec((c, tile), lambda i, s: (0, i)),
            scratch_shapes=[pltpu.VMEM((c, depth), jnp.bfloat16), pltpu.SemaphoreType.DMA((2 * n,))],
        ),
        out_shape=jax.ShapeDtypeStruct((c, 2 * held), jnp.bfloat16),
        compiler_params=pltpu.CompilerParams(vmem_limit_bytes=20 << 20, dimension_semantics=("arbitrary",)),
        cost_estimate=pl.CostEstimate(
            flops=4 * c * depth * held,
            bytes_accessed=2 * (c * depth + 2 * held * depth + 2 * c * held),
            transcendentals=0,
        ),
        name="project",
    )(inner, *flat, mine, theirs)


def expand(order, near, outs, chip_rows):
    c, depth = near.shape
    half = depth // 2
    steps = 4

    def kernel(order_ref, near_ref, own_ref, far_ref, give_ref, keep_ref):
        got = lax.dot_general(near_ref[:, :half], own_ref[...], NT, preferred_element_type=jnp.float32)
        got += lax.dot_general(near_ref[:, half:], far_ref[...], NT, preferred_element_type=jnp.float32)
        got = got.astype(jnp.bfloat16)
        step = pl.program_id(0)

        @pl.when(step < 2)
        def _():
            give_ref[0] = got

        @pl.when(step >= 2)
        def _():
            keep_ref[0] = got

    return pl.pallas_call(
        kernel,
        grid_spec=pltpu.PrefetchScalarGridSpec(
            num_scalar_prefetch=1,
            grid=(steps,),
            in_specs=[
                pl.BlockSpec((c, depth), lambda i, o: (0, 0)),
                pl.BlockSpec((chip_rows, half), lambda i, o: (o[2 + i], 0)),
                pl.BlockSpec((chip_rows, half), lambda i, o: (o[2 + i], 0)),
            ],
            out_specs=[
                pl.BlockSpec((1, c, chip_rows), lambda i, o: (jnp.minimum(i, 1), 0, 0)),
                pl.BlockSpec((1, c, chip_rows), lambda i, o: (jnp.maximum(i - 2, 0), 0, 0)),
            ],
        ),
        out_shape=[jax.ShapeDtypeStruct((2, c, chip_rows), jnp.bfloat16)] * 2,
        compiler_params=pltpu.CompilerParams(vmem_limit_bytes=12 << 20, dimension_semantics=("arbitrary",)),
        cost_estimate=pl.CostEstimate(
            flops=2 * c * depth * chip_rows * steps,
            bytes_accessed=2 * (c * depth + steps * (chip_rows * depth + c * chip_rows)),
            transcendentals=0,
        ),
        name="expand",
    )(order, near, *outs)


def hand_over(start, parts, counts, window):
    width = window // LANES
    c = parts[0].shape[0]
    sources = sum(counts) // c

    def kernel(start_ref, *refs):
        out_ref = refs[-1]
        row = 0
        for ref in refs[:-1]:
            n = ref.shape[0]
            out_ref[row // c, row % c : row % c + n, :] = ref[...]
            row += n

    return pl.pallas_call(
        kernel,
        grid_spec=pltpu.PrefetchScalarGridSpec(
            num_scalar_prefetch=1,
            grid=(width,),
            in_specs=[pl.BlockSpec((n, LANES), lambda i, s: (0, s[12] + i)) for n in counts],
            out_specs=pl.BlockSpec((sources, c, LANES), lambda i, s: (0, 0, i)),
        ),
        out_shape=jax.ShapeDtypeStruct((sources, c, window), parts[0].dtype),
        compiler_params=pltpu.CompilerParams(vmem_limit_bytes=8 << 20, dimension_semantics=("arbitrary",)),
        cost_estimate=pl.CostEstimate(flops=0, bytes_accessed=4 * sources * c * window, transcendentals=0),
        name="hand_over",
    )(start, *parts)


def mix(info, weight, kept, given, own_rows, window, first, held, columns):
    sources = given[0].shape[0]
    rels = sources
    counts = [[part.shape[0] for part in row] for row in kept]
    flat_parts = [part for row in kept for part in row]
    unit = 2 * held
    slots = 4
    targets = weight.shape[0]
    tall = 2 * slots * held
    pieces = len(PIECES)

    def kernel(info_ref, w_ref, *refs):
        total = len(flat_parts)
        flat = refs[:total]
        got = refs[total : total + pieces]
        out_ref, own, other, acc, turned, sems = refs[total + pieces :]
        step = pl.program_id(0)
        me, core = info_ref[6], info_ref[7]
        lane = pl.multiple_of(core * first, LANES)

        def copies(ring):
            for p, units in enumerate(PIECES):
                for u, (rel, kind) in enumerate(units):
                    for d in range(sources):
                        if rel ^ d != ring:
                            continue
                        yield pltpu.make_async_copy(
                            got[p].at[d, pl.ds(u * unit, unit)],
                            other.at[rel, d, pl.ds(kind * unit, unit)],
                            sems.at[ring],
                        )
                        want = d * len(units) * unit + u * unit
                        row = 0
                        for k, n in enumerate(counts[p]):
                            lo, hi = max(want, row), min(want + unit, row + n)
                            if lo < hi:
                                yield pltpu.make_async_copy(
                                    flat[sum(map(len, counts[:p])) + k].at[pl.ds(lo - row, hi - lo), pl.ds(lane, window)],
                                    own.at[rel, d, pl.ds(kind * unit + lo - want, hi - lo)],
                                    sems.at[ring],
                                )
                            row += n

        @pl.when(step == 0)
        def _():
            for ring in range(rels):
                for copy in copies(ring):
                    copy.start()

        for ring in range(rels):

            @pl.when(step == ring)
            def _():
                for copy in copies(ring):
                    copy.wait()

        for s in range(slots):
            z = info_ref[8 + s]
            for which in range(2):
                held_at = own if which == 0 else other
                base = z * unit + (core if which == 0 else 1 - core) * held
                base = pl.multiple_of(base, PACK)
                sums = [None] * targets
                for d in range(sources):
                    rel = step ^ d
                    value = held_at[rel, d, s * held : (s + 1) * held, :].astype(jnp.float32)
                    for t in range(targets):
                        term = value * w_ref[t, me ^ d]
                        sums[t] = term if d == 0 else sums[t] + term
                for t in range(targets):
                    acc[t, pl.ds(base, held), :] = sums[t]
        shift = pl.multiple_of(core * (own_rows - first), PACK)
        for t in range(targets):
            turned[...] = acc[t].T
            out_ref[t] = turned[pl.ds(shift, own_rows), :]

    return pl.pallas_call(
        kernel,
        grid_spec=pltpu.PrefetchScalarGridSpec(
            num_scalar_prefetch=2,
            grid=(rels,),
            in_specs=[pl.BlockSpec(memory_space=pl.ANY)] * (len(flat_parts) + pieces),
            out_specs=pl.BlockSpec((targets, own_rows, tall), lambda i, a, b: (0, 0, i ^ a[6])),
            scratch_shapes=[
                pltpu.VMEM((rels, sources, slots * held, window), jnp.bfloat16),
                pltpu.VMEM((rels, sources, slots * held, window), jnp.bfloat16),
                pltpu.VMEM((targets, tall, window), jnp.float32),
                pltpu.VMEM((window, tall), jnp.float32),
                pltpu.SemaphoreType.DMA((rels,)),
            ],
        ),
        out_shape=jax.ShapeDtypeStruct((targets, own_rows, columns), jnp.float32),
        compiler_params=pltpu.CompilerParams(dimension_semantics=("arbitrary",)),
        name="mix",
    )(info, weight, *flat_parts, *given)


def fold_plan(source, expand_out, expand_in, depth):
    cores = 2
    layers, width = lax.axis_size("layer"), lax.axis_size("width")
    chips = width // cores
    moves = Moves(layers, chips, cores)
    me, w = lax.axis_index("layer"), lax.axis_index("width")
    z, core = w // cores, w % cores
    rows, columns = expand_out.shape[0], expand_in.shape[0] * layers * width
    own_rows, chip_rows = rows // width, rows // chips
    window = -(-own_rows // LANES) * LANES
    first = chip_rows - window
    h = expand_in.shape[0]
    right = z >= chips // 2
    inner = jnp.logical_and(z > 0, z < chips - 1)

    pair = lambda v: moves.send(v, lambda k, z, c: (k, z ^ 1, c))
    middle = lambda v: moves.send(v, lambda k, z, c: (k, 3 - z if z in (1, 2) else z, c))
    mirror = lambda v: moves.send(v, lambda k, z, c: (k, 3 - z, c))
    over_x = lambda v: moves.across(v, 0)
    over_y = lambda v: moves.across(v, 1)
    partner = moves.partner

    mine = source.reshape(source.shape[0] * source.shape[1], source.shape[2])
    own = expand_in
    near_z = pair(own)
    mid_a = middle(own)
    x0, y0 = over_x(own), over_y(own)
    theirs = partner(mine)
    outs = (expand_out, partner(expand_out))
    mid_b = middle(near_z)
    out_b = pair(mid_a)
    x1, y1 = over_x(near_z), over_y(near_z)
    choose = lambda a, b: jnp.where(inner, a, b)
    third = choose(mid_a, out_b)
    out_c = pair(mid_b)
    x2, y2 = over_x(third), over_y(third)
    fourth = choose(mid_b, out_c)
    x3, y3 = over_x(fourth), over_y(fourth)
    d0, d2 = over_x(jnp.where(inner, y0, y1)), over_y(x2)
    d1, d3 = over_x(jnp.where(inner, y1, y0)), over_y(x3)
    held = [(own, near_z, third, fourth), (x0, x1, x2, x3), (y0, y1, y2, y3)]

    def unit(rel, kind):
        if rel == 3:
            return (d0, d0, d2) if kind == 0 else (d1, d1, d3)
        a, b, c, d = held[rel]
        return (a, b, c) if kind == 0 else (b, a, d)

    flip = lambda m: jnp.where(right, chips - 1 - m, m)
    ints = lambda *v: jnp.stack([jnp.asarray(x, jnp.int32) for x in v])
    blocks = [flip(jnp.where(inner, m, e)) for m, e in ((0, 1), (3, 2), (1, 0), (2, 3))]
    table = ints(inner, right, *blocks, me, core, 1, 2, 0, 3, jnp.where(core == 0, first // LANES, 0))
    f32 = jnp.float32

    kept, given = [], []
    for i, piece in enumerate(PIECES):
        near = project([unit(*u) for u in piece], h, table, mine, theirs)
        give, keep = expand(table, near, outs, chip_rows)
        got = pair(give)
        last = mirror((keep[1].astype(f32) + got[1].astype(f32)).astype(jnp.bfloat16))
        expanded = (keep[0].astype(f32) + got[0].astype(f32) + last.astype(f32)).astype(jnp.bfloat16)
        from_x, from_y = over_x(expanded), over_y(expanded)
        if i < len(PIECES) - 2:
            diagonal = [over_x(from_y) if i % 2 == 0 else over_y(from_x)]
        else:
            cut = expanded.shape[0] // 2
            diagonal = [over_x(from_y[:cut]), over_y(from_x[cut:])]
        spread = [expanded, from_x, from_y, *diagonal]
        give = hand_over(table, spread, [part.shape[0] for part in spread], window)
        kept.append(spread)
        given.append(partner(give))

    return mix(table, depth, kept, given, own_rows, window, first, h, columns)


def on_device(source, expand_out, expand_in, depth):
    chips = lax.axis_size("width") // 2
    aligned = expand_in.shape[0] % PACK == 0 and expand_out.shape[0] % (chips * LANES) == 0
    plan = fold_plan if chips == 4 and lax.axis_size("layer") == 4 and aligned else spread_plan
    return plan(source, expand_out, expand_in, depth)


def solution(mesh):
    return jax.shard_map(
        on_device,
        mesh=mesh,
        in_specs=(
            P("layer", "width", None),
            P(None, "width"),
            P(("layer", "width"), None),
            P("layer", None),
        ),
        out_specs=P("layer", "width", None),
        check_vma=False,
    )
```
